128 devices in a mesh: energy: 8 (over y, core), layer: 16 (over x, z).
Axes of the slice: x: 4, y: 4, z: 4, core: 2. Of those that a mesh axis runs over, the one named last changes fastest.
Arguments:
- correlations: bfloat16 [128, 16, 4, 256, 256], P(('energy', 'layer')), may hold values from -6 to 6
- retarded: bfloat16 [128, 16, 2, 256, 256], P(('energy', 'layer')), may hold values from -0.15625 to 0.15625
- coupling: bfloat16 [16, 256, 256], P('layer'), may hold values from -0.375 to 0.375
- phonon_shifts: int32 [4], replicated, may hold values from 1 to 4, as said below
- phonon_coupling: float32 [4], replicated, may hold values from 0.3 to 1.2
- layer_orbitals: int32 [16], P('layer'), may hold values from 128 to 256, as said below
Outputs:
- left_correlations: bfloat16 [128, 16, 4, 256, 256], P('energy', 'layer')
The draws below stay inside these ranges and needn't reach their ends.
Inputs may be any that keep to these rules, and one draw needn't show every extreme that they name: `phonon_shifts`: one of the offsets equals 4. `layer_orbitals`: some layer has all 256 orbitals live.
All inputs are finite; a program needn't handle non-finite values.
Results may differ from the reference program's by a relative error of at most 0.025.
Values may be sent and summed in bfloat16 or wider, within the bound.
No kernel may reach another device: no remote copies, remote signals or barrier semaphores. Data moves between devices by JAX's collectives and lax.ppermute only.
A program may use at most 128 MiB of HBM per device.

```python
import math
import jax
import jax.numpy as jnp
from jax import lax

ORBITALS = 256
MODES = 4
SHIFT_MAX = 4
ENERGIES = 128
LAYERS = 16


def draw_phonon_shifts(key, part):
    first_key, second = jax.random.split(key)
    values = jax.random.randint(first_key, (MODES,), 1, SHIFT_MAX + 1)
    chosen = jax.random.randint(second, (), 0, MODES)
    return jnp.where(jnp.arange(MODES) == chosen, SHIFT_MAX, values).astype(jnp.int32)


def draw_layer_orbitals(key, part):
    first_key, second = jax.random.split(jax.random.fold_in(key, 7))
    values = jax.random.randint(first_key, (LAYERS,), ORBITALS // 2, ORBITALS + 1)
    chosen = jax.random.randint(second, (), 0, LAYERS)
    return jnp.where(jnp.arange(LAYERS) == chosen, ORBITALS, values).astype(jnp.int32)


def steps_of(rng, dims, shards, low, largest):
    def one(position, shards_of):
        heights = jax.random.uniform(jax.random.fold_in(jax.random.fold_in(rng, 6), position), (shards_of,), jnp.float32, low / len(shards), largest / len(shards))
        return jnp.repeat(jnp.exp(heights), dims[position] // shards_of).reshape((-1,) + (1,) * (len(dims) - position - 1))

    gain = one(*shards[0])
    for cut in shards[1:]:
        gain = gain * one(*cut)
    return gain


def noise(own_key, extent, scale, bound, cuts=(), held_as=jnp.bfloat16):
    values = scale * jax.random.normal(own_key, extent, jnp.float32)
    if cuts:
        values = values * steps_of(own_key, extent, cuts, -0.22, 0.18)
    return jnp.clip(values, -bound, bound).astype(held_as)


def setup_inputs(seed: int = 0) -> dict:
    key_list = jax.random.split(jax.random.key(seed), 7)
    correlations = noise(key_list[0], (ENERGIES, LAYERS, 4, ORBITALS, ORBITALS), 1.0, 6.0, ((0, 128),))
    retarded = noise(key_list[1], (ENERGIES, LAYERS, 2, ORBITALS, ORBITALS), (ORBITALS * 6) ** -0.5, 0.15625, ((0, 128),))
    coupling = noise(key_list[2], (LAYERS, ORBITALS, ORBITALS), ORBITALS ** -0.5, 0.375, ((0, 16),))
    phonon_shifts = draw_phonon_shifts(jax.random.fold_in(key_list[6], 71), 0)
    phonon_coupling = jnp.clip(jnp.exp(jax.random.uniform(key_list[4], (MODES,), jnp.float32, math.log(0.3), math.log(1.2))), 0.3, 1.2)
    layer_orbitals = draw_layer_orbitals(jax.random.fold_in(key_list[6], 71), 0)
    return dict(correlations=correlations, retarded=retarded, coupling=coupling, phonon_shifts=phonon_shifts, phonon_coupling=phonon_coupling, layer_orbitals=layer_orbitals)


bose_ratio = 0.5


def mode_weights(shift_value):
    occupation = 1.0 / (jnp.exp(bose_ratio * shift_value.astype(jnp.float32)) - 1.0)
    lower_weight = jnp.stack([occupation, occupation, occupation + 1.0, occupation + 1.0])
    upper_weight = jnp.stack([occupation + 1.0, occupation + 1.0, occupation, occupation])
    return lower_weight, upper_weight


def self_energy(piece_block, phonon_shifts, phonon_coupling, live_count):
    padded = jnp.pad(piece_block, ((SHIFT_MAX, SHIFT_MAX), (0, 0), (0, 0), (0, 0)))
    accumulated = jnp.zeros(piece_block.shape, jnp.float32)
    for mode_index in range(MODES):
        shift_value = phonon_shifts[mode_index]
        lower_weight, upper_weight = mode_weights(shift_value)
        lower_block = lax.dynamic_slice_in_dim(padded, (SHIFT_MAX - shift_value).astype(jnp.int32), ENERGIES, 0).astype(jnp.float32)
        upper_block = lax.dynamic_slice_in_dim(padded, (SHIFT_MAX + shift_value).astype(jnp.int32), ENERGIES, 0).astype(jnp.float32)
        accumulated = accumulated + phonon_coupling[mode_index] * (lower_weight[:, None, None] * lower_block + upper_weight[:, None, None] * upper_block)
    orbital_index = jnp.arange(ORBITALS, dtype=jnp.int32)
    live_mask = (orbital_index[:, None] < live_count) & (orbital_index[None, :] < live_count)
    return jnp.where(live_mask, accumulated, 0.0).astype(jnp.bfloat16)


def rounded(values):
    return lax.optimization_barrier(values.astype(jnp.bfloat16)).astype(jnp.float32)


def advance(previous, sigma_block, green_block, coupling_block):
    wide = jnp.float32
    coupling_wide = coupling_block.astype(wide)
    halfway = rounded(jnp.einsum('...kab,cb->...kac', previous.astype(wide), coupling_wide))
    spread = jnp.einsum('ab,...kbc->...kac', coupling_wide, halfway)
    source = rounded(sigma_block.astype(wide) + spread)
    green_real = green_block[..., 0, :, :].astype(wide)
    green_imag = green_block[..., 1, :, :].astype(wide)
    source_real = source[..., 0::2, :, :]
    source_imag = source[..., 1::2, :, :]
    inner_real = rounded(jnp.einsum('...ab,...kbc->...kac', green_real, source_real) - jnp.einsum('...ab,...kbc->...kac', green_imag, source_imag))
    inner_imag = rounded(jnp.einsum('...ab,...kbc->...kac', green_real, source_imag) + jnp.einsum('...ab,...kbc->...kac', green_imag, source_real))
    outer_real = jnp.einsum('...kab,...cb->...kac', inner_real, green_real) + jnp.einsum('...kab,...cb->...kac', inner_imag, green_imag)
    outer_imag = jnp.einsum('...kab,...cb->...kac', inner_imag, green_real) - jnp.einsum('...kab,...cb->...kac', inner_real, green_imag)
    stacked = jnp.stack([outer_real, outer_imag], axis=-3)
    return stacked.reshape(stacked.shape[:-4] + (4, ORBITALS, ORBITALS)).astype(jnp.bfloat16)


def reference(correlations, retarded, coupling, phonon_shifts, phonon_coupling, layer_orbitals):
    def layer_step(previous, layer_index):
        piece_block = lax.dynamic_index_in_dim(correlations, layer_index, 1, keepdims=False)
        live_count = lax.dynamic_index_in_dim(layer_orbitals, layer_index, 0, keepdims=False)
        sigma_block = self_energy(piece_block, phonon_shifts, phonon_coupling, live_count)
        green_block = lax.dynamic_index_in_dim(retarded, layer_index, 1, keepdims=False)
        coupling_block = lax.dynamic_index_in_dim(coupling, layer_index, 0, keepdims=False)
        current = advance(previous, sigma_block, green_block, coupling_block)
        return current, current

    lead_block = correlations[:, 0]
    _, layers = lax.scan(layer_step, lead_block, jnp.arange(LAYERS, dtype=jnp.int32))
    return jnp.moveaxis(layers, 0, 1)
```

```python
import functools

import jax
import jax.numpy as jnp
from jax import lax
from jax.experimental import pallas as pl
from jax.experimental.pallas import tpu as pltpu
from jax.sharding import PartitionSpec as P

SHIFT_MAX = 4
BOSE_RATIO = 0.5
ROWS = 64


def tap_weights(phonon_shifts, phonon_coupling):
    occupation = 1.0 / (jnp.exp(BOSE_RATIO * phonon_shifts.astype(jnp.float32)) - 1.0)
    distance = jnp.arange(1, SHIFT_MAX + 1, dtype=jnp.int32)
    hit = (phonon_shifts[None, :] == distance[:, None]).astype(jnp.float32)
    absorbed = jnp.sum(hit * (phonon_coupling * occupation)[None, :], axis=1)
    emitted = jnp.sum(hit * (phonon_coupling * (occupation + 1.0))[None, :], axis=1)
    lesser = jnp.concatenate([absorbed[::-1], emitted])
    greater = jnp.concatenate([emitted[::-1], absorbed])
    return jnp.stack([lesser, greater])


def sigma_kernel(pair, weights, live, low, here, high, out):
    energies = here.shape[0]
    rows, columns = here.shape[2], here.shape[3]
    taps = [weights[pair, k] for k in range(2 * SHIFT_MAX)]
    offsets = [k - SHIFT_MAX if k < SHIFT_MAX else k - SHIFT_MAX + 1 for k in range(2 * SHIFT_MAX)]
    first_row = pl.program_id(1) * rows
    step = 16

    def block(position, carry):
        start = pl.multiple_of(position * step, step)
        row = lax.broadcasted_iota(jnp.int32, (step, columns), 0) + (first_row + start)
        column = lax.broadcasted_iota(jnp.int32, (step, columns), 1)
        mask = (row < live[0]) & (column < live[0])

        def load(energy):
            if energy < 0:
                ref, index = low, energy + SHIFT_MAX
            elif energy >= energies:
                ref, index = high, energy - energies
            else:
                ref, index = here, energy
            return ref[index, 0, pl.ds(start, step), :].astype(jnp.float32)

        for energy in range(energies):
            total = taps[0] * load(energy + offsets[0])
            for tap, offset in zip(taps[1:], offsets[1:]):
                total = total + tap * load(energy + offset)
            out[energy, 0, pl.ds(start, step), :] = jnp.where(mask, total, 0.0).astype(jnp.bfloat16)
        return carry

    lax.fori_loop(0, rows // step, block, 0)


def self_energy(pair, weights, live, low, here, high):
    energies, parts, orbitals, _ = here.shape
    halo = pl.BlockSpec((SHIFT_MAX, 1, ROWS, orbitals), lambda c, r: (0, c, r, 0))
    full = pl.BlockSpec((energies, 1, ROWS, orbitals), lambda c, r: (0, c, r, 0))
    scalar = pl.BlockSpec(memory_space=pltpu.SMEM)
    return pl.pallas_call(
        functools.partial(sigma_kernel, pair),
        grid=(parts, orbitals // ROWS),
        in_specs=[scalar, scalar, halo, full, halo],
        out_specs=full,
        out_shape=jax.ShapeDtypeStruct(here.shape, jnp.bfloat16),
        cost_estimate=pl.CostEstimate(
            flops=16 * here.size, bytes_accessed=5 * here.size, transcendentals=0
        ),
        name=f"self_energy_{pair}",
    )(weights, live, low, here, high)


def dot(left, right):
    return jnp.dot(left, right, preferred_element_type=jnp.float32)


def dot_transposed(left, right):
    return lax.dot_general(
        left, right, (((1,), (1,)), ((), ())), preferred_element_type=jnp.float32
    )


def sweep_kernel(lead, sigma, green, coupling, out, held):
    orbitals = green.shape[-1]

    @pl.when(pl.program_id(0) == 0)
    def _():
        held[...] = lead[0].reshape(2 * orbitals, orbitals)

    v = coupling[...].reshape(orbitals, orbitals)
    halfway = dot_transposed(held[...], v).astype(jnp.bfloat16)
    g_real, g_imag = green[0, 0], green[0, 1]
    source_real = (sigma[0, 0].astype(jnp.float32) + dot(v, halfway[:orbitals])).astype(jnp.bfloat16)
    source_imag = (sigma[0, 1].astype(jnp.float32) + dot(v, halfway[orbitals:])).astype(jnp.bfloat16)
    inner_real = (dot(g_real, source_real) - dot(g_imag, source_imag)).astype(jnp.bfloat16)
    inner_imag = (dot(g_real, source_imag) + dot(g_imag, source_real)).astype(jnp.bfloat16)
    outer_real = (dot_transposed(inner_real, g_real) + dot_transposed(inner_imag, g_imag)).astype(jnp.bfloat16)
    outer_imag = (dot_transposed(inner_imag, g_real) - dot_transposed(inner_real, g_imag)).astype(jnp.bfloat16)
    held[:orbitals] = outer_real
    held[orbitals:] = outer_imag
    out[0, 0] = outer_real
    out[0, 1] = outer_imag


def sweep(pair, correlations, sigma, green, coupling):
    layers, _, orbitals, _ = sigma.shape
    parts = coupling.shape[0]
    block = pl.BlockSpec((1, 2, orbitals, orbitals), lambda i: (i, 0, 0, 0))
    return pl.pallas_call(
        sweep_kernel,
        grid=(layers,),
        in_specs=[
            pl.BlockSpec((1, 2, orbitals, orbitals), lambda i: (0, pair, 0, 0)),
            block,
            block,
            pl.BlockSpec((parts, 1, orbitals // parts, orbitals), lambda i: (0, i, 0, 0)),
        ],
        out_specs=block,
        out_shape=jax.ShapeDtypeStruct(sigma.shape, jnp.bfloat16),
        scratch_shapes=[pltpu.VMEM((2 * orbitals, orbitals), jnp.bfloat16)],
        cost_estimate=pl.CostEstimate(
            flops=24 * layers * orbitals**3,
            bytes_accessed=14 * layers * orbitals**2,
            transcendentals=0,
        ),
        name=f"sweep_{pair}",
    )(correlations, sigma, green, coupling)


def exchange(block, axis):
    return lax.all_to_all(block, axis, split_axis=0, concat_axis=0, tiled=True)


def halo_of(block):
    count = lax.axis_size("energy")
    forward = [(i, i + 1) for i in range(count - 1)]
    backward = [(i + 1, i) for i in range(count - 1)]
    low = lax.ppermute(block[-SHIFT_MAX:], "energy", forward)
    high = lax.ppermute(block[:SHIFT_MAX], "energy", backward)
    return low, high


def all_couplings(coupling):
    layers, groups = lax.axis_size("layer"), lax.axis_size("energy")
    rows = coupling.shape[1] // groups
    piece = lax.dynamic_slice_in_dim(coupling, lax.axis_index("energy") * rows, rows, axis=1)
    pieces = exchange(jnp.broadcast_to(piece, (layers,) + piece.shape[1:]), "layer")
    return exchange(jnp.broadcast_to(pieces[None], (groups,) + pieces.shape), "energy")


def body(correlations, retarded, coupling, phonon_shifts, phonon_coupling, layer_orbitals):
    weights = tap_weights(phonon_shifts, phonon_coupling)
    mine = correlations[0]
    green = retarded[0]
    couplings = all_couplings(coupling)
    arrived = [exchange(mine[:, 2 * p : 2 * p + 2], "layer") for p in range(2)]
    outs = []
    for p in range(2):
        low, high = halo_of(arrived[p])
        sigma = self_energy(p, weights, layer_orbitals, low, arrived[p], high)
        returned = exchange(sigma, "layer")
        finished = sweep(p, mine, returned, green, couplings)
        outs.append(exchange(finished, "layer"))
    return jnp.concatenate(outs, axis=1)[:, None]


def solution(mesh):
    return jax.shard_map(
        body,
        mesh=mesh,
        in_specs=(
            P(("energy", "layer"), None, None, None, None),
            P(("energy", "layer"), None, None, None, None),
            P("layer", None, None),
            P(),
            P(),
            P("layer"),
        ),
        out_specs=P("energy", "layer", None, None, None),
        check_vma=False,
    )
```

```python
import functools

import jax
import jax.numpy as jnp
from jax import lax
from jax.experimental import pallas as pl
from jax.experimental.pallas import tpu as pltpu
from jax.sharding import PartitionSpec as P

SHIFT_MAX = 4
BOSE_RATIO = 0.5
ROWS = 64
ENERGY_BITS = (2, 4, 1)
ENERGY_OFFSETS = tuple(
    sum(bit for place, bit in enumerate(ENERGY_BITS) if k >> place & 1) for k in range(8)
)


def tap_weights(phonon_shifts, phonon_coupling):
    occupation = 1.0 / (jnp.exp(BOSE_RATIO * phonon_shifts.astype(jnp.float32)) - 1.0)
    distance = jnp.arange(1, SHIFT_MAX + 1, dtype=jnp.int32)
    hit = (phonon_shifts[None, :] == distance[:, None]).astype(jnp.float32)
    absorbed = jnp.sum(hit * (phonon_coupling * occupation)[None, :], axis=1)
    emitted = jnp.sum(hit * (phonon_coupling * (occupation + 1.0))[None, :], axis=1)
    lesser = jnp.concatenate([absorbed[::-1], emitted])
    greater = jnp.concatenate([emitted[::-1], absorbed])
    return jnp.stack([lesser, greater])


def sigma_kernel(pair, weights, live, low, here, high, out):
    energies = here.shape[0]
    rows, columns = here.shape[2], here.shape[3]
    taps = [weights[pair, k] for k in range(2 * SHIFT_MAX)]
    offsets = [k - SHIFT_MAX if k < SHIFT_MAX else k - SHIFT_MAX + 1 for k in range(2 * SHIFT_MAX)]
    first_row = pl.program_id(1) * rows
    step = 16

    def block(position, carry):
        start = pl.multiple_of(position * step, step)
        row = lax.broadcasted_iota(jnp.int32, (step, columns), 0) + (first_row + start)
        column = lax.broadcasted_iota(jnp.int32, (step, columns), 1)
        mask = (row < live[0]) & (column < live[0])

        def load(energy):
            if energy < 0:
                ref, index = low, energy + SHIFT_MAX
            elif energy >= energies:
                ref, index = high, energy - energies
            else:
                ref, index = here, energy
            return ref[index, 0, pl.ds(start, step), :].astype(jnp.float32)

        for energy in range(energies):
            total = taps[0] * load(energy + offsets[0])
            for tap, offset in zip(taps[1:], offsets[1:]):
                total = total + tap * load(energy + offset)
            out[energy, 0, pl.ds(start, step), :] = jnp.where(mask, total, 0.0).astype(jnp.bfloat16)
        return carry

    lax.fori_loop(0, rows // step, block, 0)


def self_energy(pair, weights, live, low, here, high):
    energies, parts, orbitals, _ = here.shape
    halo = pl.BlockSpec((SHIFT_MAX, 1, ROWS, orbitals), lambda c, r: (0, c, r, 0))
    full = pl.BlockSpec((energies, 1, ROWS, orbitals), lambda c, r: (0, c, r, 0))
    scalar = pl.BlockSpec(memory_space=pltpu.SMEM)
    return pl.pallas_call(
        functools.partial(sigma_kernel, pair),
        grid=(parts, orbitals // ROWS),
        in_specs=[scalar, scalar, halo, full, halo],
        out_specs=full,
        out_shape=jax.ShapeDtypeStruct(here.shape, jnp.bfloat16),
        cost_estimate=pl.CostEstimate(
            flops=16 * here.size, bytes_accessed=5 * here.size, transcendentals=0
        ),
        name=f"self_energy_{pair}",
    )(weights, live, low, here, high)


def dot(left, right):
    return jnp.dot(left, right, preferred_element_type=jnp.float32)


def dot_transposed(left, right):
    return lax.dot_general(
        left, right, (((1,), (1,)), ((), ())), preferred_element_type=jnp.float32
    )


def sweep_kernel(place, lead, sigma, green, coupling, out, held, matrix):
    orbitals = green.shape[-1]
    rows = coupling.shape[2]
    for k, offset in enumerate(ENERGY_OFFSETS):
        group = place[0] ^ offset
        matrix[pl.ds(pl.multiple_of(group * rows, rows), rows), :] = coupling[k, 0]

    @pl.when(pl.program_id(0) == 0)
    def _():
        held[...] = lead[0].reshape(2 * orbitals, orbitals)

    v = matrix[...]
    halfway = dot_transposed(held[...], v).astype(jnp.bfloat16)
    g_real, g_imag = green[0, 0], green[0, 1]
    source_real = (sigma[0, 0].astype(jnp.float32) + dot(v, halfway[:orbitals])).astype(jnp.bfloat16)
    source_imag = (sigma[0, 1].astype(jnp.float32) + dot(v, halfway[orbitals:])).astype(jnp.bfloat16)
    inner_real = (dot(g_real, source_real) - dot(g_imag, source_imag)).astype(jnp.bfloat16)
    inner_imag = (dot(g_real, source_imag) + dot(g_imag, source_real)).astype(jnp.bfloat16)
    outer_real = (dot_transposed(inner_real, g_real) + dot_transposed(inner_imag, g_imag)).astype(jnp.bfloat16)
    outer_imag = (dot_transposed(inner_imag, g_real) - dot_transposed(inner_real, g_imag)).astype(jnp.bfloat16)
    held[:orbitals] = outer_real
    held[orbitals:] = outer_imag
    out[0, 0] = outer_real
    out[0, 1] = outer_imag


def sweep(pair, place, correlations, sigma, green, coupling):
    layers, _, orbitals, _ = sigma.shape
    parts = coupling.shape[0]
    block = pl.BlockSpec((1, 2, orbitals, orbitals), lambda i, place: (i, 0, 0, 0))
    return pl.pallas_call(
        sweep_kernel,
        grid_spec=pltpu.PrefetchScalarGridSpec(
            num_scalar_prefetch=1,
            grid=(layers,),
            in_specs=[
                pl.BlockSpec((1, 2, orbitals, orbitals), lambda i, place: (0, pair, 0, 0)),
                block,
                block,
                pl.BlockSpec(
                    (parts, 1, orbitals // parts, orbitals), lambda i, place: (0, i ^ place[1], 0, 0)
                ),
            ],
            out_specs=block,
            scratch_shapes=[
                pltpu.VMEM((2 * orbitals, orbitals), jnp.bfloat16),
                pltpu.VMEM((orbitals, orbitals), jnp.bfloat16),
            ],
        ),
        out_shape=jax.ShapeDtypeStruct(sigma.shape, jnp.bfloat16),
        cost_estimate=pl.CostEstimate(
            flops=24 * layers * orbitals**3,
            bytes_accessed=14 * layers * orbitals**2,
            transcendentals=0,
        ),
        name=f"sweep_{pair}",
    )(place, correlations, sigma, green, coupling)


def copy_kernel(source, *rest):
    rest[-1][...] = source[...]


def pick_pair(pair, blocks):
    layers, parts, orbitals, _ = blocks.shape
    half = parts // 2
    group = 2
    return pl.pallas_call(
        copy_kernel,
        grid=(layers // group,),
        in_specs=[pl.BlockSpec((group, half, orbitals, orbitals), lambda i: (i, pair, 0, 0))],
        out_specs=pl.BlockSpec((group, half, orbitals, orbitals), lambda i: (i, 0, 0, 0)),
        out_shape=jax.ShapeDtypeStruct((layers, half, orbitals, orbitals), blocks.dtype),
        cost_estimate=pl.CostEstimate(flops=0, bytes_accessed=2 * blocks.size, transcendentals=0),
        name=f"pick_{pair}",
    )(blocks)


def place_pair(pair, blocks, whole=None):
    layers, half, orbitals, _ = blocks.shape
    group = 2
    shape = (layers, 1, 2 * half, orbitals, orbitals)
    in_specs = [pl.BlockSpec((group, half, orbitals, orbitals), lambda i: (i, 0, 0, 0))]
    if whole is not None:
        in_specs.append(pl.BlockSpec(memory_space=pl.ANY))
    return pl.pallas_call(
        lambda source, *rest: rest[-1].__setitem__((slice(None), 0), source[...]),
        grid=(layers // group,),
        in_specs=in_specs,
        out_specs=pl.BlockSpec((group, 1, half, orbitals, orbitals), lambda i: (i, 0, pair, 0, 0)),
        out_shape=jax.ShapeDtypeStruct(shape, blocks.dtype),
        input_output_aliases={} if whole is None else {1: 0},
        cost_estimate=pl.CostEstimate(flops=0, bytes_accessed=4 * blocks.size, transcendentals=0),
        name=f"place_{pair}",
    )(*((blocks,) if whole is None else (blocks, whole)))


def exchange(block, axis):
    return lax.all_to_all(block, axis, split_axis=0, concat_axis=0, tiled=True)


def halo_of(block):
    count = lax.axis_size("energy")
    forward = [(i, i + 1) for i in range(count - 1)]
    backward = [(i + 1, i) for i in range(count - 1)]
    low = lax.ppermute(block[-SHIFT_MAX:], "energy", forward)
    high = lax.ppermute(block[:SHIFT_MAX], "energy", backward)
    return low, high


def swapped(block, axis, bit):
    count = lax.axis_size(axis)
    return lax.ppermute(block, axis, [(i, i ^ bit) for i in range(count)])


def couplings_of_line(coupling):
    layers, groups = lax.axis_size("layer"), lax.axis_size("energy")
    rows = coupling.shape[1] // groups
    held = lax.dynamic_slice_in_dim(coupling, lax.axis_index("energy") * rows, rows, axis=1)
    bit = 1
    while bit < layers:
        held = jnp.concatenate([held, swapped(held, "layer", bit)], axis=0)
        bit *= 2
    return held[None]


def doubled(held, bits):
    for bit in bits:
        held = jnp.concatenate([held, swapped(held, "energy", bit)], axis=0)
    return held


def body(correlations, retarded, coupling, phonon_shifts, phonon_coupling, layer_orbitals):
    weights = tap_weights(phonon_shifts, phonon_coupling)
    place = jnp.stack([lax.axis_index("energy"), lax.axis_index("layer")]).astype(jnp.int32)
    mine = correlations[0]
    green = retarded[0]
    picked, coupling = lax.optimization_barrier((pick_pair(1, mine), coupling))
    held = doubled(couplings_of_line(coupling), ENERGY_BITS[:1])
    picked, held = lax.optimization_barrier((picked, held))
    arrived = [exchange(block, "layer") for block in (pick_pair(0, mine), picked)]
    couplings = doubled(held, ENERGY_BITS[1:])
    whole = None
    for p in range(2):
        low, high = halo_of(arrived[p])
        sigma = self_energy(p, weights, layer_orbitals, low, arrived[p], high)
        if p == 0:
            sigma, couplings = lax.optimization_barrier((sigma, couplings))
        returned = exchange(sigma, "layer")
        finished = sweep(p, place, mine, returned, green, couplings)
        whole = place_pair(p, exchange(finished, "layer"), whole)
    return whole


def solution(mesh):
    return jax.shard_map(
        body,
        mesh=mesh,
        in_specs=(
            P(("energy", "layer"), None, None, None, None),
            P(("energy", "layer"), None, None, None, None),
            P("layer", None, None),
            P(),
            P(),
            P("layer"),
        ),
        out_specs=P("energy", "layer", None, None, None),
        check_vma=False,
    )
```

```python
import functools
import math

import jax
import jax.numpy as jnp
from jax import lax
from jax.experimental import pallas as pl
from jax.experimental.pallas import tpu as pltpu
from jax.sharding import PartitionSpec as P

SHIFT_MAX = 4
BOSE_RATIO = 0.5
ROWS = 64
ENERGY_BITS = (2, 4, 1)
ENERGY_OFFSETS = tuple(
    sum(bit for place, bit in enumerate(ENERGY_BITS) if k >> place & 1) for k in range(8)
)


def tap_weights(phonon_shifts, phonon_coupling):
    occupation = 1.0 / (jnp.exp(BOSE_RATIO * phonon_shifts.astype(jnp.float32)) - 1.0)
    distance = jnp.arange(1, SHIFT_MAX + 1, dtype=jnp.int32)
    hit = (phonon_shifts[None, :] == distance[:, None]).astype(jnp.float32)
    absorbed = jnp.sum(hit * (phonon_coupling * occupation)[None, :], axis=1)
    emitted = jnp.sum(hit * (phonon_coupling * (occupation + 1.0))[None, :], axis=1)
    lesser = jnp.concatenate([absorbed[::-1], emitted])
    greater = jnp.concatenate([emitted[::-1], absorbed])
    return jnp.stack([lesser, greater])


def sigma_kernel(pair, per_part, weights, live, low, here, high, out):
    energies, rows, columns = here.shape
    taps = [weights[pair, k] for k in range(2 * SHIFT_MAX)]
    offsets = [k - SHIFT_MAX if k < SHIFT_MAX else k - SHIFT_MAX + 1 for k in range(2 * SHIFT_MAX)]
    first_row = lax.rem(pl.program_id(0), per_part) * rows
    step = 16

    def block(position, carry):
        start = pl.multiple_of(position * step, step)
        row = lax.broadcasted_iota(jnp.int32, (step, columns), 0) + (first_row + start)
        column = lax.broadcasted_iota(jnp.int32, (step, columns), 1)
        mask = (row < live[0]) & (column < live[0])

        def load(energy):
            if energy < 0:
                ref, index = low, energy + SHIFT_MAX
            elif energy >= energies:
                ref, index = high, energy - energies
            else:
                ref, index = here, energy
            return ref[index, pl.ds(start, step), :].astype(jnp.float32)

        for energy in range(energies):
            total = taps[0] * load(energy + offsets[0])
            for tap, offset in zip(taps[1:], offsets[1:]):
                total = total + tap * load(energy + offset)
            out[energy, pl.ds(start, step), :] = jnp.where(mask, total, 0.0).astype(jnp.bfloat16)
        return carry

    lax.fori_loop(0, rows // step, block, 0)


def self_energy(pair, weights, live, low, here, high):
    energies, _, orbitals = here.shape
    per_part = orbitals // ROWS
    halo = pl.BlockSpec((SHIFT_MAX, ROWS, orbitals), lambda r: (0, r, 0))
    full = pl.BlockSpec((energies, ROWS, orbitals), lambda r: (0, r, 0))
    scalar = pl.BlockSpec(memory_space=pltpu.SMEM)
    shape = (energies, 2 * orbitals, orbitals)
    size = math.prod(shape)
    return pl.pallas_call(
        functools.partial(sigma_kernel, pair, per_part),
        grid=(2 * per_part,),
        in_specs=[scalar, scalar, halo, full, halo],
        out_specs=full,
        out_shape=jax.ShapeDtypeStruct(shape, jnp.bfloat16),
        cost_estimate=pl.CostEstimate(flops=16 * size, bytes_accessed=5 * size, transcendentals=0),
        name=f"self_energy_{pair}",
    )(weights, live, low, here, high)


def dot(left, right):
    return jnp.dot(left, right, preferred_element_type=jnp.float32)


def dot_transposed(left, right):
    return lax.dot_general(
        left, right, (((1,), (1,)), ((), ())), preferred_element_type=jnp.float32
    )


def sweep_kernel(place, lead, sigma, green, coupling, out, held, matrix):
    orbitals = green.shape[-1]
    rows = coupling.shape[2]
    for k, offset in enumerate(ENERGY_OFFSETS):
        group = place[0] ^ offset
        matrix[pl.ds(pl.multiple_of(group * rows, rows), rows), :] = coupling[k, 0]

    @pl.when(pl.program_id(0) == 0)
    def _():
        held[...] = lead[0]

    v = matrix[...]
    halfway = dot_transposed(held[...], v).astype(jnp.bfloat16)
    g_real, g_imag = green[0, 0], green[0, 1]
    wide = jnp.float32
    source_real = (sigma[0, :orbitals].astype(wide) + dot(v, halfway[:orbitals])).astype(jnp.bfloat16)
    source_imag = (sigma[0, orbitals:].astype(wide) + dot(v, halfway[orbitals:])).astype(jnp.bfloat16)
    inner_real = (dot(g_real, source_real) - dot(g_imag, source_imag)).astype(jnp.bfloat16)
    inner_imag = (dot(g_real, source_imag) + dot(g_imag, source_real)).astype(jnp.bfloat16)
    outer_real = (dot_transposed(inner_real, g_real) + dot_transposed(inner_imag, g_imag)).astype(jnp.bfloat16)
    outer_imag = (dot_transposed(inner_imag, g_real) - dot_transposed(inner_real, g_imag)).astype(jnp.bfloat16)
    held[:orbitals] = outer_real
    held[orbitals:] = outer_imag
    out[0, :orbitals] = outer_real
    out[0, orbitals:] = outer_imag


def sweep(pair, place, flat, sigma, green, coupling):
    layers, both, orbitals = sigma.shape
    parts = coupling.shape[0]
    block = pl.BlockSpec((1, both, orbitals), lambda i, place: (i, 0, 0))
    return pl.pallas_call(
        sweep_kernel,
        grid_spec=pltpu.PrefetchScalarGridSpec(
            num_scalar_prefetch=1,
            grid=(layers,),
            in_specs=[
                pl.BlockSpec((1, both, orbitals), lambda i, place: (0, pair, 0)),
                block,
                pl.BlockSpec((1, 2, orbitals, orbitals), lambda i, place: (i, 0, 0, 0)),
                pl.BlockSpec((parts, 1, orbitals // parts, orbitals), lambda i, place: (0, i, 0, 0)),
            ],
            out_specs=block,
            scratch_shapes=[
                pltpu.VMEM((both, orbitals), jnp.bfloat16),
                pltpu.VMEM((orbitals, orbitals), jnp.bfloat16),
            ],
        ),
        out_shape=jax.ShapeDtypeStruct(sigma.shape, jnp.bfloat16),
        cost_estimate=pl.CostEstimate(
            flops=24 * layers * orbitals**3,
            bytes_accessed=14 * layers * orbitals**2,
            transcendentals=0,
        ),
        name=f"sweep_{pair}",
    )(place, flat, sigma, green, coupling)


def relay(sources, slots, targets, arrived, gone):
    fetches = [
        pltpu.make_async_copy(source, slot, arrived.at[k])
        for k, (source, slot) in enumerate(zip(sources, slots))
    ]
    puts = [
        pltpu.make_async_copy(slot, target, gone.at[k])
        for k, (slot, target) in enumerate(zip(slots, targets))
    ]
    for fetch in fetches:
        fetch.start()
    for fetch, put in zip(fetches, puts):
        fetch.wait()
        put.start()
    for put in puts:
        put.wait()


def relay_scratch(layers, rows, orbitals):
    return [
        pltpu.VMEM((layers, rows, orbitals), jnp.bfloat16),
        pltpu.SemaphoreType.DMA((layers,)),
        pltpu.SemaphoreType.DMA((layers,)),
    ]


def pick_kernel(pair, blocks, out, held, arrived, gone):
    layers, rows = held.shape[:2]
    relay(
        [blocks.at[i, pl.ds(pair * rows, rows)] for i in range(layers)],
        [held.at[i] for i in range(layers)],
        [out.at[i, pl.ds(0, rows)] for i in range(layers)],
        arrived,
        gone,
    )


def pick_with_coupling_kernel(pair, blocks, coupling, out, held, arrived, gone, piece, here, sent):
    layers, rows = held.shape[:2]
    extra = piece.shape[0]
    group = lax.axis_index("energy")
    own = pl.ds(pl.multiple_of(group * extra, extra), extra)
    fetch = pltpu.make_async_copy(coupling.at[0, own], piece, here)
    fetch.start()
    pick_kernel(pair, blocks, out, held, arrived, gone)
    fetch.wait()
    puts = [
        pltpu.make_async_copy(piece, out.at[i, pl.ds(rows, extra)], sent.at[i]) for i in range(layers)
    ]
    for put in puts:
        put.start()
    for put in puts:
        put.wait()


def pick_pair(pair, flat, coupling=None):
    layers, rows, orbitals = flat.shape
    rows //= 2
    extra = 0
    kernel = functools.partial(pick_kernel, pair)
    operands, scratch = [flat], relay_scratch(layers, rows, orbitals)
    if coupling is not None:
        extra = orbitals // lax.axis_size("energy")
        kernel = functools.partial(pick_with_coupling_kernel, pair)
        operands.append(coupling)
        scratch += [
            pltpu.VMEM((extra, orbitals), jnp.bfloat16),
            pltpu.SemaphoreType.DMA(()),
            pltpu.SemaphoreType.DMA((layers,)),
        ]
    return pl.pallas_call(
        kernel,
        in_specs=[pl.BlockSpec(memory_space=pl.ANY)] * len(operands),
        out_specs=pl.BlockSpec(memory_space=pl.ANY),
        out_shape=jax.ShapeDtypeStruct((layers, rows + extra, orbitals), flat.dtype),
        scratch_shapes=scratch,
        cost_estimate=pl.CostEstimate(flops=0, bytes_accessed=2 * flat.size, transcendentals=0),
        name=f"pick_{pair}",
    )(*operands)


def place_kernel(pair, blocks, *rest):
    out, held, arrived, gone = rest[-4:]
    layers, rows = held.shape[:2]
    relay(
        [blocks.at[i] for i in range(layers)],
        [held.at[i] for i in range(layers)],
        [out.at[i, pl.ds(pair * rows, rows)] for i in range(layers)],
        arrived,
        gone,
    )


def place_pair(pair, blocks, whole=None):
    layers, rows, orbitals = blocks.shape
    operands = (blocks,) if whole is None else (blocks, whole)
    return pl.pallas_call(
        functools.partial(place_kernel, pair),
        in_specs=[pl.BlockSpec(memory_space=pl.ANY)] * len(operands),
        out_specs=pl.BlockSpec(memory_space=pl.ANY),
        out_shape=jax.ShapeDtypeStruct((layers, 2 * rows, orbitals), blocks.dtype),
        scratch_shapes=relay_scratch(layers, rows, orbitals),
        input_output_aliases={} if whole is None else {1: 0},
        cost_estimate=pl.CostEstimate(flops=0, bytes_accessed=4 * blocks.size, transcendentals=0),
        name=f"place_{pair}",
    )(*operands)


def exchange(block):
    return lax.all_to_all(block, "layer", split_axis=0, concat_axis=0, tiled=True)


def halo_of(block):
    count = lax.axis_size("energy")
    forward = [(i, i + 1) for i in range(count - 1)]
    backward = [(i + 1, i) for i in range(count - 1)]
    low = lax.ppermute(block[-SHIFT_MAX:], "energy", forward)
    high = lax.ppermute(block[:SHIFT_MAX], "energy", backward)
    return low, high


def all_couplings(held):
    count = lax.axis_size("energy")
    held = held[None]
    for bit in ENERGY_BITS:
        other = lax.ppermute(held, "energy", [(i, i ^ bit) for i in range(count)])
        held = jnp.concatenate([held, other], axis=0)
    return held


def body(correlations, retarded, coupling, phonon_shifts, phonon_coupling, layer_orbitals):
    weights = tap_weights(phonon_shifts, phonon_coupling)
    place = jnp.stack([lax.axis_index("energy"), lax.axis_index("layer")]).astype(jnp.int32)
    layers, parts, orbitals = correlations.shape[1:4]
    flat = correlations.reshape(layers, parts * orbitals, orbitals)
    rows = parts * orbitals // 2
    picked = lax.optimization_barrier([pick_pair(0, flat, coupling), pick_pair(1, flat)])
    arrived = [exchange(block) for block in picked]
    couplings = all_couplings(arrived[0][:, rows:])
    whole = None
    for p in range(2):
        low, high = halo_of(arrived[p][:, :rows])
        sigma = self_energy(p, weights, layer_orbitals, low, arrived[p], high)
        if p == 0:
            sigma, couplings = lax.optimization_barrier((sigma, couplings))
        finished = sweep(p, place, flat, exchange(sigma), retarded[0], couplings)
        whole = place_pair(p, exchange(finished), whole)
    return whole.reshape(layers, 1, parts, orbitals, orbitals)


def solution(mesh):
    return jax.shard_map(
        body,
        mesh=mesh,
        in_specs=(
            P(("energy", "layer"), None, None, None, None),
            P(("energy", "layer"), None, None, None, None),
            P("layer", None, None),
            P(),
            P(),
            P("layer"),
        ),
        out_specs=P("energy", "layer", None, None, None),
        check_vma=False,
    )
```

```python
import functools
import math

import jax
import jax.numpy as jnp
from jax import lax
from jax.experimental import pallas as pl
from jax.experimental.pallas import tpu as pltpu
from jax.sharding import PartitionSpec as P

SHIFT_MAX = 4
BOSE_RATIO = 0.5
FIRST_LAYERS = 10
LIVE_ROWS = 16
ENERGY_BITS = (2, 4, 1)
ENERGY_OFFSETS = tuple(
    sum(bit for place, bit in enumerate(ENERGY_BITS) if k >> place & 1) for k in range(8)
)


def tap_weights(phonon_shifts, phonon_coupling):
    occupation = 1.0 / (jnp.exp(BOSE_RATIO * phonon_shifts.astype(jnp.float32)) - 1.0)
    distance = jnp.arange(1, SHIFT_MAX + 1, dtype=jnp.int32)
    hit = (phonon_shifts[None, :] == distance[:, None]).astype(jnp.float32)
    absorbed = jnp.sum(hit * (phonon_coupling * occupation)[None, :], axis=1)
    emitted = jnp.sum(hit * (phonon_coupling * (occupation + 1.0))[None, :], axis=1)
    lesser = jnp.concatenate([absorbed[::-1], emitted])
    greater = jnp.concatenate([emitted[::-1], absorbed])
    return jnp.stack([lesser, greater])


def sigma_kernel(weights, low, here, high, out):
    energies, rows, columns = here.shape
    taps = [weights[k] for k in range(2 * SHIFT_MAX)]
    offsets = [k - SHIFT_MAX if k < SHIFT_MAX else k - SHIFT_MAX + 1 for k in range(2 * SHIFT_MAX)]
    step, width = 16, 128
    refs = [(low, e) for e in range(SHIFT_MAX)]
    refs += [(here, e) for e in range(energies)]
    refs += [(high, e) for e in range(SHIFT_MAX)]

    def block(position, carry):
        tile = pl.ds(pl.multiple_of(position * step, step), step)
        for left in range(0, columns, width):
            lanes = pl.ds(left, width)
            loaded = [ref[e, tile, lanes].astype(jnp.float32) for ref, e in refs]
            for energy in range(energies):
                terms = [
                    tap * loaded[energy + SHIFT_MAX + offset] for tap, offset in zip(taps, offsets)
                ]
                while len(terms) > 1:
                    terms = [x + y for x, y in zip(terms[0::2], terms[1::2])]
                out[energy, tile, lanes] = terms[0].astype(jnp.bfloat16)
        return carry

    lax.fori_loop(0, rows // step, block, 0)


def self_energy(name, weights, low, here, high, rows, share):
    energies, _, orbitals = here.shape
    halo = pl.BlockSpec((SHIFT_MAX, share, orbitals), lambda r: (0, r, 0))
    full = pl.BlockSpec((energies, share, orbitals), lambda r: (0, r, 0))
    size = energies * rows * orbitals
    return pl.pallas_call(
        sigma_kernel,
        grid=(rows // share,),
        in_specs=[pl.BlockSpec(memory_space=pltpu.SMEM), halo, full, halo],
        out_specs=full,
        out_shape=jax.ShapeDtypeStruct((energies, rows, orbitals), jnp.bfloat16),
        cost_estimate=pl.CostEstimate(flops=16 * size, bytes_accessed=5 * size, transcendentals=0),
        name=f"self_energy_{name}",
    )(weights, low, here, high)


def dot(left, right):
    return jnp.dot(left, right, preferred_element_type=jnp.float32)


def dot_transposed(left, right):
    return lax.dot_general(
        left, right, (((1,), (1,)), ((), ())), preferred_element_type=jnp.float32
    )


def sweep_kernel(first, group, live, lead, sigma, green, coupling, *rest):
    out, last, held, matrix = rest[-4:]
    narrow = jnp.bfloat16
    orbitals = green.shape[-1]
    rows = coupling.shape[2]
    layer = pl.program_id(0)
    for k, offset in enumerate(ENERGY_OFFSETS):
        start = pl.multiple_of((group[0] ^ offset) * rows, rows)
        matrix[pl.ds(start, rows), :] = coupling[k, 0]

    @pl.when(layer == 0)
    def _():
        held[...] = lead[0]

    row = lax.broadcasted_iota(jnp.int32, (orbitals, orbitals), 0)
    column = lax.broadcasted_iota(jnp.int32, (orbitals, orbitals), 1)
    mask = jnp.maximum(row, column) < live[first + layer]

    v = matrix[...]
    halfway = dot_transposed(held[...], v).astype(narrow)
    own = sigma[...].reshape(4 * orbitals, orbitals)
    source = []
    for k in range(4):
        part = slice(k * orbitals, (k + 1) * orbitals)
        spread = dot(v, halfway[part])
        source.append((jnp.where(mask, own[part].astype(jnp.float32), 0.0) + spread).astype(narrow))
    g_real, g_imag = green[0, 0], green[0, 1]
    g_minus = jnp.concatenate([g_real, -g_imag], axis=1)
    g_plus = jnp.concatenate([g_real, g_imag], axis=1)
    stacked = []
    for k in (0, 2):
        inner_real = dot(g_minus, jnp.concatenate([source[k], source[k + 1]], axis=0)).astype(narrow)
        inner_imag = dot(g_plus, jnp.concatenate([source[k + 1], source[k]], axis=0)).astype(narrow)
        stacked.append(jnp.concatenate([inner_real, inner_imag], axis=1))
        stacked.append(jnp.concatenate([inner_imag, -inner_real], axis=1))
    outer = dot_transposed(jnp.concatenate(stacked, axis=0), g_plus).astype(narrow)
    held[...] = outer
    out[0] = outer
    last[0] = outer


def sweep(first, group, live, lead, sigma, retarded, couplings, whole=None):
    layers, _, orbitals, _ = retarded.shape
    sources, rows, _ = sigma.shape
    share = 4 * orbitals // sources
    count = rows // share
    parts = couplings.shape[0]
    state = pl.BlockSpec((1, 4 * orbitals, orbitals), lambda i, group, live: (0, 0, 0))
    in_specs = [
        state,
        pl.BlockSpec((sources, share, orbitals), lambda i, group, live: (0, i, 0)),
        pl.BlockSpec((1, 2, orbitals, orbitals), lambda i, group, live: (first + i, 0, 0, 0)),
        pl.BlockSpec((parts, 1, orbitals // parts, orbitals), lambda i, group, live: (0, first + i, 0, 0)),
    ]
    operands = [group, live, lead, sigma, retarded, couplings]
    if whole is not None:
        in_specs.append(pl.BlockSpec(memory_space=pl.ANY))
        operands.append(whole)
    return pl.pallas_call(
        functools.partial(sweep_kernel, first),
        grid_spec=pltpu.PrefetchScalarGridSpec(
            num_scalar_prefetch=2,
            grid=(count,),
            in_specs=in_specs,
            out_specs=[
                pl.BlockSpec((1, 4 * orbitals, orbitals), lambda i, group, live: (first + i, 0, 0)),
                state,
            ],
            scratch_shapes=[
                pltpu.VMEM((4 * orbitals, orbitals), jnp.bfloat16),
                pltpu.VMEM((orbitals, orbitals), jnp.bfloat16),
            ],
        ),
        out_shape=[
            jax.ShapeDtypeStruct((layers, 4 * orbitals, orbitals), jnp.bfloat16),
            jax.ShapeDtypeStruct((1, 4 * orbitals, orbitals), jnp.bfloat16),
        ],
        input_output_aliases={} if whole is None else {6: 0},
        cost_estimate=pl.CostEstimate(
            flops=48 * count * orbitals**3,
            bytes_accessed=28 * count * orbitals**2,
            transcendentals=0,
        ),
        name=f"sweep_{first}",
    )(*operands)


def pick_kernel(blocks, coupling, live, first, second, arrived, here, sent):
    layers, devices, share, _ = blocks.shape
    split = first.shape[1] // share
    rows = coupling.shape[1] // lax.axis_size("energy")
    start = pl.multiple_of(lax.axis_index("energy") * rows, rows)
    tail = (layers - split) * share
    copies = []
    for i in range(layers):
        target = first if i < split else second
        where = pl.ds((i if i < split else i - split) * share, share)
        copies.append(pltpu.make_async_copy(blocks.at[i], target.at[:, where], arrived.at[i]))
    for d in range(devices):
        mine = coupling.at[0, pl.ds(start, rows)]
        copies.append(pltpu.make_async_copy(mine, second.at[d, pl.ds(tail, rows)], here.at[d]))
        target = second.at[d, pl.ds(tail + rows, LIVE_ROWS)]
        copies.append(pltpu.make_async_copy(live, target, sent.at[d]))
    for copy in copies:
        copy.start()
    for copy in copies:
        copy.wait()


def pick(blocks, coupling, live_rows):
    layers, devices, share, orbitals = blocks.shape
    rows = orbitals // lax.axis_size("energy")
    extra = rows + LIVE_ROWS
    shapes = (FIRST_LAYERS * share, (layers - FIRST_LAYERS) * share + extra)
    return pl.pallas_call(
        pick_kernel,
        in_specs=[pl.BlockSpec(memory_space=pltpu.HBM)] * 3,
        out_specs=[pl.BlockSpec(memory_space=pltpu.VMEM)] * 2,
        out_shape=[pltpu.VMEM((devices, n, orbitals), blocks.dtype) for n in shapes],
        scratch_shapes=[pltpu.SemaphoreType.DMA((n,)) for n in (layers, devices, devices)],
        cost_estimate=pl.CostEstimate(flops=0, bytes_accessed=2 * blocks.size, transcendentals=0),
        compiler_params=pltpu.CompilerParams(vmem_limit_bytes=16 << 20),
        name="pick",
    )(blocks, coupling, live_rows)


def settle_kernel(source, out, gone):
    copies = [
        pltpu.make_async_copy(source.at[i], out.at[i], gone.at[i]) for i in range(source.shape[0])
    ]
    for copy in copies:
        copy.start()
    for copy in copies:
        copy.wait()


def settle(blocks):
    return pl.pallas_call(
        settle_kernel,
        in_specs=[pl.BlockSpec(memory_space=pltpu.VMEM)],
        out_specs=pl.BlockSpec(memory_space=pl.ANY),
        out_shape=jax.ShapeDtypeStruct(blocks.shape, blocks.dtype),
        scratch_shapes=[pltpu.SemaphoreType.DMA((blocks.shape[0],))],
        cost_estimate=pl.CostEstimate(flops=0, bytes_accessed=2 * blocks.size, transcendentals=0),
        compiler_params=pltpu.CompilerParams(vmem_limit_bytes=16 << 20),
        name="settle",
    )(blocks)


def exchange(block):
    return lax.all_to_all(block, "layer", split_axis=0, concat_axis=0, tiled=True)


def exchange_into(block, space):
    return pltpu.with_memory_space_constraint(exchange(block), space)


def halo_of(block):
    count = lax.axis_size("energy")
    forward = [(i, i + 1) for i in range(count - 1)]
    backward = [(i + 1, i) for i in range(count - 1)]
    low = lax.ppermute(block[-SHIFT_MAX:], "energy", forward)
    high = lax.ppermute(block[:SHIFT_MAX], "energy", backward)
    return low, high


def all_couplings(held):
    count = lax.axis_size("energy")
    held = held[None]
    for bit in ENERGY_BITS:
        other = lax.ppermute(held, "energy", [(i, i ^ bit) for i in range(count)])
        held = jnp.concatenate([held, other], axis=0)
    return held


def body(correlations, retarded, coupling, phonon_shifts, phonon_coupling, layer_orbitals):
    layers, parts, orbitals = correlations.shape[1:4]
    devices = lax.axis_size("layer")
    share = parts * orbitals // devices
    pair = lax.axis_index("layer") * 2 // devices
    weights = lax.dynamic_index_in_dim(tap_weights(phonon_shifts, phonon_coupling), pair, 0, keepdims=False)
    group = lax.axis_index("energy").astype(jnp.int32)[None]
    live_rows = jnp.broadcast_to(layer_orbitals.astype(jnp.bfloat16)[:, None], (LIVE_ROWS, orbitals))
    picked = pick(correlations.reshape(layers, devices, share, orbitals), coupling, live_rows)
    arrived = [exchange(block) for block in picked]
    rows = (FIRST_LAYERS * share, (layers - FIRST_LAYERS) * share)
    extra = arrived[1][:, rows[1] :]
    group_rows = extra.shape[1] - LIVE_ROWS
    couplings = all_couplings(extra[:, :group_rows])
    live = extra[:, group_rows, 0].astype(jnp.int32)
    sigmas = []
    for c in range(2):
        low, high = halo_of(arrived[c][:, : rows[c]])
        sigmas.append(self_energy(c, weights, low, arrived[c], high, rows[c], share))
    sigmas[1], couplings, live = lax.optimization_barrier((sigmas[1], couplings, live))
    lead = correlations.reshape(layers, parts * orbitals, orbitals)
    returned = [exchange_into(sigma, pltpu.HBM) for sigma in sigmas]
    whole, lead = sweep(0, group, live, lead, returned[0], retarded[0], couplings)
    whole, _ = sweep(FIRST_LAYERS, group, live, lead, returned[1], retarded[0], couplings, whole)
    return settle(exchange_into(whole, pltpu.VMEM)).reshape(layers, 1, parts, orbitals, orbitals)


def solution(mesh):
    return jax.shard_map(
        body,
        mesh=mesh,
        in_specs=(
            P(("energy", "layer"), None, None, None, None),
            P(("energy", "layer"), None, None, None, None),
            P("layer", None, None),
            P(),
            P(),
            P("layer"),
        ),
        out_specs=P("energy", "layer", None, None, None),
        check_vma=False,
    )
```

```python
import functools
import math

import jax
import jax.numpy as jnp
from jax import lax
from jax.experimental import pallas as pl
from jax.experimental.pallas import tpu as pltpu
from jax.sharding import PartitionSpec as P

SHIFT_MAX = 4
BOSE_RATIO = 0.5
FIRST_LAYERS = 10
LIVE_ROWS = 8
ENERGY_BITS = (2, 4, 1)
ENERGY_OFFSETS = tuple(
    sum(bit for place, bit in enumerate(ENERGY_BITS) if k >> place & 1) for k in range(8)
)


def tap_weights(phonon_shifts, phonon_coupling):
    occupation = 1.0 / (jnp.exp(BOSE_RATIO * phonon_shifts.astype(jnp.float32)) - 1.0)
    distance = jnp.arange(1, SHIFT_MAX + 1, dtype=jnp.int32)
    hit = (phonon_shifts[None, :] == distance[:, None]).astype(jnp.float32)
    absorbed = jnp.sum(hit * (phonon_coupling * occupation)[None, :], axis=1)
    emitted = jnp.sum(hit * (phonon_coupling * (occupation + 1.0))[None, :], axis=1)
    lesser = jnp.concatenate([absorbed[::-1], emitted])
    greater = jnp.concatenate([emitted[::-1], absorbed])
    return jnp.stack([lesser, greater])


def sigma_kernel(weights, low, here, high, out):
    energies, rows, columns = here.shape
    taps = [weights[k] for k in range(2 * SHIFT_MAX)]
    offsets = [k - SHIFT_MAX if k < SHIFT_MAX else k - SHIFT_MAX + 1 for k in range(2 * SHIFT_MAX)]
    step, width = 16, 128
    refs = [(low, e) for e in range(SHIFT_MAX)]
    refs += [(here, e) for e in range(energies)]
    refs += [(high, e) for e in range(SHIFT_MAX)]

    def block(position, carry):
        tile = pl.ds(pl.multiple_of(position * step, step), step)
        for left in range(0, columns, width):
            lanes = pl.ds(left, width)
            loaded = [ref[e, tile, lanes].astype(jnp.float32) for ref, e in refs]
            for energy in range(energies):
                terms = [
                    tap * loaded[energy + SHIFT_MAX + offset] for tap, offset in zip(taps, offsets)
                ]
                while len(terms) > 1:
                    terms = [x + y for x, y in zip(terms[0::2], terms[1::2])]
                out[energy, tile, lanes] = terms[0].astype(jnp.bfloat16)
        return carry

    lax.fori_loop(0, rows // step, block, 0)


def self_energy(name, weights, low, here, high, rows, share):
    energies, _, orbitals = here.shape
    halo = pl.BlockSpec((SHIFT_MAX, share, orbitals), lambda r: (0, r, 0))
    full = pl.BlockSpec((energies, share, orbitals), lambda r: (0, r, 0))
    size = energies * rows * orbitals
    return pl.pallas_call(
        sigma_kernel,
        grid=(rows // share,),
        in_specs=[pl.BlockSpec(memory_space=pltpu.SMEM), halo, full, halo],
        out_specs=full,
        out_shape=jax.ShapeDtypeStruct((energies, rows, orbitals), jnp.bfloat16),
        cost_estimate=pl.CostEstimate(flops=16 * size, bytes_accessed=5 * size, transcendentals=0),
        name=f"self_energy_{name}",
    )(weights, low, here, high)


def dot(left, right):
    return jnp.dot(left, right, preferred_element_type=jnp.float32)


def dot_transposed(left, right):
    return lax.dot_general(
        left, right, (((1,), (1,)), ((), ())), preferred_element_type=jnp.float32
    )


def sweep_kernel(first, group, live, lead, sigma, green, coupling, *rest):
    out, last, held, matrix = rest[-4:]
    narrow = jnp.bfloat16
    orbitals = green.shape[-1]
    rows = coupling.shape[2]
    layer = pl.program_id(0)
    for k, offset in enumerate(ENERGY_OFFSETS):
        start = pl.multiple_of((group[0] ^ offset) * rows, rows)
        matrix[pl.ds(start, rows), :] = coupling[k, 0]

    @pl.when(layer == 0)
    def _():
        held[...] = lead[0]

    row = lax.broadcasted_iota(jnp.int32, (orbitals, orbitals), 0)
    column = lax.broadcasted_iota(jnp.int32, (orbitals, orbitals), 1)
    mask = jnp.maximum(row, column) < live[first + layer]

    v = matrix[...]
    halfway = dot_transposed(held[...], v).astype(narrow)
    share = 4 * orbitals // sigma.shape[0]
    if sigma.shape[1] == share:
        own = sigma[...]
    else:
        own = sigma[:, pl.ds(pl.multiple_of(layer * share, share), share), :]
    own = own.reshape(4 * orbitals, orbitals)
    source = []
    for k in range(4):
        part = slice(k * orbitals, (k + 1) * orbitals)
        spread = dot(v, halfway[part])
        source.append((jnp.where(mask, own[part].astype(jnp.float32), 0.0) + spread).astype(narrow))
    g_real, g_imag = green[0, 0], green[0, 1]
    g_minus = jnp.concatenate([g_real, -g_imag], axis=1)
    g_plus = jnp.concatenate([g_real, g_imag], axis=1)
    stacked = []
    for k in (0, 2):
        inner_real = dot(g_minus, jnp.concatenate([source[k], source[k + 1]], axis=0)).astype(narrow)
        inner_imag = dot(g_plus, jnp.concatenate([source[k + 1], source[k]], axis=0)).astype(narrow)
        stacked.append(jnp.concatenate([inner_real, inner_imag], axis=1))
        stacked.append(jnp.concatenate([inner_imag, -inner_real], axis=1))
    outer = dot_transposed(jnp.concatenate(stacked, axis=0), g_plus).astype(narrow)
    held[...] = outer
    out[0] = outer
    last[0] = outer


def sweep(first, group, live, lead, sigma, retarded, couplings, whole=None):
    layers, _, orbitals, _ = retarded.shape
    sources, rows, _ = sigma.shape
    share = 4 * orbitals // sources
    count = rows // share
    parts = couplings.shape[0]
    state = pl.BlockSpec((1, 4 * orbitals, orbitals), lambda i, group, live: (0, 0, 0))
    in_specs = [
        state,
        pl.BlockSpec((sources, share, orbitals), lambda i, group, live: (0, i, 0))
        if whole is None
        else pl.BlockSpec(memory_space=pltpu.VMEM),
        pl.BlockSpec((1, 2, orbitals, orbitals), lambda i, group, live: (first + i, 0, 0, 0)),
        pl.BlockSpec((parts, 1, orbitals // parts, orbitals), lambda i, group, live: (0, first + i, 0, 0)),
    ]
    operands = [group, live, lead, sigma, retarded, couplings]
    if whole is not None:
        in_specs.append(pl.BlockSpec(memory_space=pl.ANY))
        operands.append(whole)
    return pl.pallas_call(
        functools.partial(sweep_kernel, first),
        grid_spec=pltpu.PrefetchScalarGridSpec(
            num_scalar_prefetch=2,
            grid=(count,),
            in_specs=in_specs,
            out_specs=[
                pl.BlockSpec((1, 4 * orbitals, orbitals), lambda i, group, live: (first + i, 0, 0)),
                state,
            ],
            scratch_shapes=[
                pltpu.VMEM((4 * orbitals, orbitals), jnp.bfloat16),
                pltpu.VMEM((orbitals, orbitals), jnp.bfloat16),
            ],
        ),
        out_shape=[
            pltpu.HBM((layers, 4 * orbitals, orbitals), jnp.bfloat16),
            pltpu.HBM((1, 4 * orbitals, orbitals), jnp.bfloat16),
        ],
        input_output_aliases={} if whole is None else {6: 0},
        cost_estimate=pl.CostEstimate(
            flops=48 * count * orbitals**3,
            bytes_accessed=28 * count * orbitals**2,
            transcendentals=0,
        ),
        compiler_params=pltpu.CompilerParams(vmem_limit_bytes=24 << 20),
        name=f"sweep_{first}",
    )(*operands)


def pick_kernel(blocks, coupling, live, first, second, held, extra, arrived, gone, here, sent):
    layers, devices, share, _ = blocks.shape
    split = first.shape[1] // share
    count = layers - split
    rows = extra.shape[0] - LIVE_ROWS
    start = pl.multiple_of(lax.axis_index("energy") * rows, rows)
    extras = [
        pltpu.make_async_copy(coupling.at[0, pl.ds(start, rows)], extra.at[pl.ds(0, rows)], here.at[0]),
        pltpu.make_async_copy(live, extra.at[pl.ds(rows, LIVE_ROWS)], here.at[1]),
    ]
    tails = [
        pltpu.make_async_copy(extra, second.at[d, pl.ds(count * share, rows + LIVE_ROWS)], sent.at[d])
        for d in range(devices)
    ]
    fetches = [
        pltpu.make_async_copy(blocks.at[split + i], held.at[i], arrived.at[i]) for i in range(count)
    ]
    puts = [
        pltpu.make_async_copy(held.at[i], second.at[:, pl.ds(i * share, share)], gone.at[i])
        for i in range(count)
    ]
    direct = [
        pltpu.make_async_copy(blocks.at[i], first.at[:, pl.ds(i * share, share)], arrived.at[count + i])
        for i in range(split)
    ]
    for copy in extras + fetches + direct:
        copy.start()
    for copy in extras:
        copy.wait()
    for copy in tails:
        copy.start()
    for fetch, put in zip(fetches, puts):
        fetch.wait()
        put.start()
    for copy in direct + tails + puts:
        copy.wait()


def pick(blocks, coupling, live_rows):
    layers, devices, share, orbitals = blocks.shape
    count = layers - FIRST_LAYERS
    extra = orbitals // lax.axis_size("energy") + LIVE_ROWS
    return pl.pallas_call(
        pick_kernel,
        in_specs=[pl.BlockSpec(memory_space=pltpu.HBM)] * 3,
        out_specs=[pl.BlockSpec(memory_space=pltpu.VMEM), pl.BlockSpec(memory_space=pltpu.HBM)],
        out_shape=[
            pltpu.VMEM((devices, FIRST_LAYERS * share, orbitals), blocks.dtype),
            pltpu.HBM((devices, count * share + extra, orbitals), blocks.dtype),
        ],
        scratch_shapes=[
            pltpu.VMEM((count, devices, share, orbitals), blocks.dtype),
            pltpu.VMEM((extra, orbitals), blocks.dtype),
            pltpu.SemaphoreType.DMA((layers,)),
            pltpu.SemaphoreType.DMA((count,)),
            pltpu.SemaphoreType.DMA((2,)),
            pltpu.SemaphoreType.DMA((devices,)),
        ],
        cost_estimate=pl.CostEstimate(flops=0, bytes_accessed=4 * blocks.size, transcendentals=0),
        compiler_params=pltpu.CompilerParams(vmem_limit_bytes=16 << 20),
        name="pick",
    )(blocks, coupling, live_rows)


def settle_kernel(source, out, gone):
    copies = [
        pltpu.make_async_copy(source.at[i], out.at[i], gone.at[i]) for i in range(source.shape[0])
    ]
    for copy in copies:
        copy.start()
    for copy in copies:
        copy.wait()


def settle(blocks):
    return pl.pallas_call(
        settle_kernel,
        in_specs=[pl.BlockSpec(memory_space=pltpu.VMEM)],
        out_specs=pl.BlockSpec(memory_space=pl.ANY),
        out_shape=jax.ShapeDtypeStruct(blocks.shape, blocks.dtype),
        scratch_shapes=[pltpu.SemaphoreType.DMA((blocks.shape[0],))],
        cost_estimate=pl.CostEstimate(flops=0, bytes_accessed=2 * blocks.size, transcendentals=0),
        compiler_params=pltpu.CompilerParams(vmem_limit_bytes=16 << 20),
        name="settle",
    )(blocks)


def exchange(block):
    return lax.all_to_all(block, "layer", split_axis=0, concat_axis=0, tiled=True)


def in_hbm(array):
    return pltpu.with_memory_space_constraint(array, pltpu.HBM)


def exchange_into(block, space):
    return pltpu.with_memory_space_constraint(exchange(block), space)


def halo_of(block):
    count = lax.axis_size("energy")
    forward = [(i, i + 1) for i in range(count - 1)]
    backward = [(i + 1, i) for i in range(count - 1)]
    low = lax.ppermute(block[-SHIFT_MAX:], "energy", forward)
    high = lax.ppermute(block[:SHIFT_MAX], "energy", backward)
    return low, high


def all_couplings(held):
    count = lax.axis_size("energy")
    held = held[None]
    for bit in ENERGY_BITS:
        other = lax.ppermute(held, "energy", [(i, i ^ bit) for i in range(count)])
        held = jnp.concatenate([held, other], axis=0)
    return held


def body(correlations, retarded, coupling, phonon_shifts, phonon_coupling, layer_orbitals):
    layers, parts, orbitals = correlations.shape[1:4]
    devices = lax.axis_size("layer")
    share = parts * orbitals // devices
    pair = lax.axis_index("layer") * 2 // devices
    weights = lax.dynamic_index_in_dim(tap_weights(phonon_shifts, phonon_coupling), pair, 0, keepdims=False)
    group = lax.axis_index("energy").astype(jnp.int32)[None]
    live_rows = jnp.broadcast_to(layer_orbitals.astype(jnp.bfloat16)[:, None], (LIVE_ROWS, orbitals))
    blocks = correlations.reshape(layers, devices, share, orbitals)
    picked = pick(in_hbm(blocks), in_hbm(coupling), live_rows)
    arrived = [exchange(block) for block in picked]
    rows = (FIRST_LAYERS * share, (layers - FIRST_LAYERS) * share)
    extra = arrived[1][:, rows[1] :]
    group_rows = extra.shape[1] - LIVE_ROWS
    couplings = all_couplings(extra[:, :group_rows])
    live = extra[:, group_rows, 0].astype(jnp.int32)
    sigmas = []
    for c in range(2):
        low, high = halo_of(arrived[c][:, : rows[c]])
        sigmas.append(self_energy(c, weights, low, arrived[c], high, rows[c], share))
    sigmas[1], couplings, live = lax.optimization_barrier((sigmas[1], couplings, live))
    lead = in_hbm(correlations.reshape(layers, parts * orbitals, orbitals))
    green, couplings = in_hbm(retarded[0]), in_hbm(couplings)
    spaces = (pltpu.HBM, pltpu.VMEM)
    returned = [exchange_into(sigma, space) for sigma, space in zip(sigmas, spaces)]
    whole, lead = sweep(0, group, live, lead, returned[0], green, couplings)
    whole, _ = sweep(FIRST_LAYERS, group, live, in_hbm(lead), returned[1], green, couplings, whole)
    return settle(exchange_into(whole, pltpu.VMEM)).reshape(layers, 1, parts, orbitals, orbitals)


def solution(mesh):
    return jax.shard_map(
        body,
        mesh=mesh,
        in_specs=(
            P(("energy", "layer"), None, None, None, None),
            P(("energy", "layer"), None, None, None, None),
            P("layer", None, None),
            P(),
            P(),
            P("layer"),
        ),
        out_specs=P("energy", "layer", None, None, None),
        check_vma=False,
    )
```

```python
import functools
import math

import jax
import jax.numpy as jnp
from jax import lax
from jax.experimental import pallas as pl
from jax.experimental.pallas import tpu as pltpu
from jax.sharding import PartitionSpec as P

SHIFT_MAX = 4
BOSE_RATIO = 0.5
FIRST_LAYERS = 10
LIVE_ROWS = 8
ENERGY_BITS = (2, 4, 1)
ENERGY_OFFSETS = tuple(
    sum(bit for place, bit in enumerate(ENERGY_BITS) if k >> place & 1) for k in range(8)
)


def tap_weights(phonon_shifts, phonon_coupling):
    occupation = 1.0 / (jnp.exp(BOSE_RATIO * phonon_shifts.astype(jnp.float32)) - 1.0)
    distance = jnp.arange(1, SHIFT_MAX + 1, dtype=jnp.int32)
    hit = (phonon_shifts[None, :] == distance[:, None]).astype(jnp.float32)
    absorbed = jnp.sum(hit * (phonon_coupling * occupation)[None, :], axis=1)
    emitted = jnp.sum(hit * (phonon_coupling * (occupation + 1.0))[None, :], axis=1)
    lesser = jnp.concatenate([absorbed[::-1], emitted])
    greater = jnp.concatenate([emitted[::-1], absorbed])
    return jnp.stack([lesser, greater])


def sigma_kernel(weights, low, here, high, out):
    energies, rows, columns = here.shape
    taps = [weights[k] for k in range(2 * SHIFT_MAX)]
    offsets = [k - SHIFT_MAX if k < SHIFT_MAX else k - SHIFT_MAX + 1 for k in range(2 * SHIFT_MAX)]
    step, width = 16, 128
    refs = [(low, e) for e in range(SHIFT_MAX)]
    refs += [(here, e) for e in range(energies)]
    refs += [(high, e) for e in range(SHIFT_MAX)]

    def block(position, carry):
        tile = pl.ds(pl.multiple_of(position * step, step), step)
        for left in range(0, columns, width):
            lanes = pl.ds(left, width)
            loaded = [ref[e, tile, lanes].astype(jnp.float32) for ref, e in refs]
            for energy in range(energies):
                terms = [
                    tap * loaded[energy + SHIFT_MAX + offset] for tap, offset in zip(taps, offsets)
                ]
                while len(terms) > 1:
                    terms = [x + y for x, y in zip(terms[0::2], terms[1::2])]
                out[energy, tile, lanes] = terms[0].astype(jnp.bfloat16)
        return carry

    lax.fori_loop(0, rows // step, block, 0)


def self_energy(name, weights, low, here, high, rows, share):
    energies, _, orbitals = here.shape
    halo = pl.BlockSpec((SHIFT_MAX, share, orbitals), lambda r: (0, r, 0))
    full = pl.BlockSpec((energies, share, orbitals), lambda r: (0, r, 0))
    size = energies * rows * orbitals
    return pl.pallas_call(
        sigma_kernel,
        grid=(rows // share,),
        in_specs=[pl.BlockSpec(memory_space=pltpu.SMEM), halo, full, halo],
        out_specs=full,
        out_shape=jax.ShapeDtypeStruct((energies, rows, orbitals), jnp.bfloat16),
        cost_estimate=pl.CostEstimate(flops=16 * size, bytes_accessed=5 * size, transcendentals=0),
        name=f"self_energy_{name}",
    )(weights, low, here, high)


def dot(left, right):
    return jnp.dot(left, right, preferred_element_type=jnp.float32)


def dot_transposed(left, right):
    return lax.dot_general(
        left, right, (((1,), (1,)), ((), ())), preferred_element_type=jnp.float32
    )


def sweep_kernel(first, group, live, lead, sigma, green, coupling, *rest):
    last = rest[1] if first == 0 else None
    out, held, matrix = rest[0] if first == 0 else rest[1], rest[-2], rest[-1]
    narrow = jnp.bfloat16
    orbitals = green.shape[-1]
    rows = coupling.shape[2]
    layer = pl.program_id(0)
    for k, offset in enumerate(ENERGY_OFFSETS):
        start = pl.multiple_of((group[0] ^ offset) * rows, rows)
        matrix[pl.ds(start, rows), :] = coupling[k, 0]

    @pl.when(layer == 0)
    def _():
        held[...] = lead[0]

    row = lax.broadcasted_iota(jnp.int32, (orbitals, orbitals), 0)
    column = lax.broadcasted_iota(jnp.int32, (orbitals, orbitals), 1)
    mask = jnp.maximum(row, column) < live[first + layer]

    v = matrix[...]
    halfway = dot_transposed(held[...], v).astype(narrow)
    share = 4 * orbitals // sigma.shape[0]
    if sigma.shape[1] == share:
        own = sigma[...]
    else:
        own = sigma[:, pl.ds(pl.multiple_of(layer * share, share), share), :]
    own = own.reshape(4 * orbitals, orbitals)
    source = []
    for k in range(4):
        part = slice(k * orbitals, (k + 1) * orbitals)
        spread = dot(v, halfway[part])
        source.append((jnp.where(mask, own[part].astype(jnp.float32), 0.0) + spread).astype(narrow))
    g_real, g_imag = green[0, 0], green[0, 1]
    g_minus = jnp.concatenate([g_real, -g_imag], axis=1)
    g_plus = jnp.concatenate([g_real, g_imag], axis=1)
    stacked = []
    for k in (0, 2):
        inner_real = dot(g_minus, jnp.concatenate([source[k], source[k + 1]], axis=0)).astype(narrow)
        inner_imag = dot(g_plus, jnp.concatenate([source[k + 1], source[k]], axis=0)).astype(narrow)
        stacked.append(jnp.concatenate([inner_real, inner_imag], axis=1))
        stacked.append(jnp.concatenate([inner_imag, -inner_real], axis=1))
    outer = dot_transposed(jnp.concatenate(stacked, axis=0), g_plus).astype(narrow)
    held[...] = outer
    out[0] = outer
    if last is not None:
        last[0] = outer


def sweep(first, layers, group, live, lead, sigma, green, couplings, whole=None):
    orbitals = green.shape[-1]
    sources, rows, _ = sigma.shape
    share = 4 * orbitals // sources
    count = rows // share
    parts = couplings.shape[0]
    state = pl.BlockSpec((1, 4 * orbitals, orbitals), lambda i, group, live: (0, 0, 0))
    output = pl.BlockSpec((1, 4 * orbitals, orbitals), lambda i, group, live: (first + i, 0, 0))
    operands = [group, live, lead, sigma, green, couplings]
    out_specs, out_shape = [output], [pltpu.HBM((layers, 4 * orbitals, orbitals), jnp.bfloat16)]
    in_specs = [
        state,
        pl.BlockSpec((sources, share, orbitals), lambda i, group, live: (0, i, 0)),
        pl.BlockSpec((1, 2, orbitals, orbitals), lambda i, group, live: (first + i, 0, 0, 0)),
        pl.BlockSpec((parts, 1, orbitals // parts, orbitals), lambda i, group, live: (0, first + i, 0, 0)),
    ]
    if whole is None:
        out_specs.append(state)
        out_shape.append(pltpu.HBM((1, 4 * orbitals, orbitals), jnp.bfloat16))
    else:
        in_specs[1] = pl.BlockSpec(memory_space=pltpu.VMEM)
        in_specs.append(pl.BlockSpec(memory_space=pl.ANY))
        operands.append(whole)
    return pl.pallas_call(
        functools.partial(sweep_kernel, first),
        grid_spec=pltpu.PrefetchScalarGridSpec(
            num_scalar_prefetch=2,
            grid=(count,),
            in_specs=in_specs,
            out_specs=out_specs,
            scratch_shapes=[
                pltpu.VMEM((4 * orbitals, orbitals), jnp.bfloat16),
                pltpu.VMEM((orbitals, orbitals), jnp.bfloat16),
            ],
        ),
        out_shape=out_shape,
        input_output_aliases={} if whole is None else {6: 0},
        cost_estimate=pl.CostEstimate(
            flops=48 * count * orbitals**3,
            bytes_accessed=28 * count * orbitals**2,
            transcendentals=0,
        ),
        compiler_params=pltpu.CompilerParams(vmem_limit_bytes=24 << 20),
        name=f"sweep_{first}",
    )(*operands)


def pick_kernel(blocks, coupling, live, first, second, held, extra, arrived, gone, here, sent):
    layers, devices, share, _ = blocks.shape
    split = first.shape[1] // share
    count = layers - split
    rows = extra.shape[0] - LIVE_ROWS
    start = pl.multiple_of(lax.axis_index("energy") * rows, rows)
    extras = [
        pltpu.make_async_copy(coupling.at[0, pl.ds(start, rows)], extra.at[pl.ds(0, rows)], here.at[0]),
        pltpu.make_async_copy(live, extra.at[pl.ds(rows, LIVE_ROWS)], here.at[1]),
    ]
    tails = [
        pltpu.make_async_copy(extra, second.at[d, pl.ds(count * share, rows + LIVE_ROWS)], sent.at[d])
        for d in range(devices)
    ]
    fetches = [
        pltpu.make_async_copy(blocks.at[split + i], held.at[i], arrived.at[i]) for i in range(count)
    ]
    puts = [
        pltpu.make_async_copy(held.at[i], second.at[:, pl.ds(i * share, share)], gone.at[i])
        for i in range(count)
    ]
    direct = [
        pltpu.make_async_copy(blocks.at[i], first.at[:, pl.ds(i * share, share)], arrived.at[count + i])
        for i in range(split)
    ]
    for copy in extras + fetches + direct:
        copy.start()
    for copy in extras:
        copy.wait()
    for copy in tails:
        copy.start()
    for fetch, put in zip(fetches, puts):
        fetch.wait()
        put.start()
    for copy in direct + tails + puts:
        copy.wait()


def pick(blocks, coupling, live_rows):
    layers, devices, share, orbitals = blocks.shape
    count = layers - FIRST_LAYERS
    extra = orbitals // lax.axis_size("energy") + LIVE_ROWS
    return pl.pallas_call(
        pick_kernel,
        in_specs=[pl.BlockSpec(memory_space=pltpu.HBM)] * 3,
        out_specs=[pl.BlockSpec(memory_space=pltpu.VMEM), pl.BlockSpec(memory_space=pltpu.HBM)],
        out_shape=[
            pltpu.VMEM((devices, FIRST_LAYERS * share, orbitals), blocks.dtype),
            pltpu.HBM((devices, count * share + extra, orbitals), blocks.dtype),
        ],
        scratch_shapes=[
            pltpu.VMEM((count, devices, share, orbitals), blocks.dtype),
            pltpu.VMEM((extra, orbitals), blocks.dtype),
            pltpu.SemaphoreType.DMA((layers,)),
            pltpu.SemaphoreType.DMA((count,)),
            pltpu.SemaphoreType.DMA((2,)),
            pltpu.SemaphoreType.DMA((devices,)),
        ],
        cost_estimate=pl.CostEstimate(flops=0, bytes_accessed=4 * blocks.size, transcendentals=0),
        compiler_params=pltpu.CompilerParams(vmem_limit_bytes=16 << 20),
        name="pick",
    )(blocks, coupling, live_rows)


def settle_kernel(source, out, gone):
    copies = [
        pltpu.make_async_copy(source.at[i], out.at[i], gone.at[i]) for i in range(source.shape[0])
    ]
    for copy in copies:
        copy.start()
    for copy in copies:
        copy.wait()


def settle(blocks):
    return pl.pallas_call(
        settle_kernel,
        in_specs=[pl.BlockSpec(memory_space=pltpu.VMEM)],
        out_specs=pl.BlockSpec(memory_space=pl.ANY),
        out_shape=jax.ShapeDtypeStruct(blocks.shape, blocks.dtype),
        scratch_shapes=[pltpu.SemaphoreType.DMA((blocks.shape[0],))],
        cost_estimate=pl.CostEstimate(flops=0, bytes_accessed=2 * blocks.size, transcendentals=0),
        compiler_params=pltpu.CompilerParams(vmem_limit_bytes=16 << 20),
        name="settle",
    )(blocks)


def exchange(block):
    return lax.all_to_all(block, "layer", split_axis=0, concat_axis=0, tiled=True)


def in_hbm(array):
    return pltpu.with_memory_space_constraint(array, pltpu.HBM)


def exchange_into(block, space):
    return pltpu.with_memory_space_constraint(exchange(block), space)


def halo_of(block):
    count = lax.axis_size("energy")
    forward = [(i, i + 1) for i in range(count - 1)]
    backward = [(i + 1, i) for i in range(count - 1)]
    low = lax.ppermute(block[-SHIFT_MAX:], "energy", forward)
    high = lax.ppermute(block[:SHIFT_MAX], "energy", backward)
    return low, high


def all_couplings(held):
    count = lax.axis_size("energy")
    held = held[None]
    for bit in ENERGY_BITS:
        other = lax.ppermute(held, "energy", [(i, i ^ bit) for i in range(count)])
        held = jnp.concatenate([held, other], axis=0)
    return held


def body(correlations, retarded, coupling, phonon_shifts, phonon_coupling, layer_orbitals):
    layers, parts, orbitals = correlations.shape[1:4]
    devices = lax.axis_size("layer")
    share = parts * orbitals // devices
    pair = lax.axis_index("layer") * 2 // devices
    weights = lax.dynamic_index_in_dim(tap_weights(phonon_shifts, phonon_coupling), pair, 0, keepdims=False)
    group = lax.axis_index("energy").astype(jnp.int32)[None]
    live_rows = jnp.broadcast_to(layer_orbitals.astype(jnp.bfloat16)[:, None], (LIVE_ROWS, orbitals))
    blocks = correlations.reshape(layers, devices, share, orbitals)
    picked = pick(in_hbm(blocks), in_hbm(coupling), live_rows)
    arrived = [exchange(block) for block in picked]
    rows = (FIRST_LAYERS * share, (layers - FIRST_LAYERS) * share)
    extra = arrived[1][:, rows[1] :]
    group_rows = extra.shape[1] - LIVE_ROWS
    couplings = all_couplings(extra[:, :group_rows])
    live = extra[:, group_rows, 0].astype(jnp.int32)
    sigmas = []
    for c in range(2):
        low, high = halo_of(arrived[c][:, : rows[c]])
        sigmas.append(self_energy(c, weights, low, arrived[c], high, rows[c], 2 * share))
    sigmas[1], couplings, live = lax.optimization_barrier((sigmas[1], couplings, live))
    lead = in_hbm(correlations.reshape(layers, parts * orbitals, orbitals))
    green, couplings = in_hbm(retarded[0]), in_hbm(couplings)
    spaces = (pltpu.HBM, pltpu.VMEM)
    returned = [exchange_into(sigma, space) for sigma, space in zip(sigmas, spaces)]
    whole, lead = sweep(0, layers, group, live, lead, returned[0], green, couplings)
    (whole,) = sweep(FIRST_LAYERS, layers, group, live, in_hbm(lead), returned[1], green, couplings, whole)
    return settle(exchange_into(whole, pltpu.VMEM)).reshape(layers, 1, parts, orbitals, orbitals)


def solution(mesh):
    return jax.shard_map(
        body,
        mesh=mesh,
        in_specs=(
            P(("energy", "layer"), None, None, None, None),
            P(("energy", "layer"), None, None, None, None),
            P("layer", None, None),
            P(),
            P(),
            P("layer"),
        ),
        out_specs=P("energy", "layer", None, None, None),
        check_vma=False,
    )
```

```python
import functools
import math

import jax
import jax.numpy as jnp
from jax import lax
from jax.experimental import pallas as pl
from jax.experimental.pallas import tpu as pltpu
from jax.sharding import PartitionSpec as P

SHIFT_MAX = 4
BOSE_RATIO = 0.5
FIRST_LAYERS = 10
LIVE_ROWS = 8
ENERGY_BITS = (2, 4, 1)
ENERGY_OFFSETS = tuple(
    sum(bit for place, bit in enumerate(ENERGY_BITS) if k >> place & 1) for k in range(8)
)


def tap_weights(phonon_shifts, phonon_coupling):
    occupation = 1.0 / (jnp.exp(BOSE_RATIO * phonon_shifts.astype(jnp.float32)) - 1.0)
    distance = jnp.arange(1, SHIFT_MAX + 1, dtype=jnp.int32)
    hit = (phonon_shifts[None, :] == distance[:, None]).astype(jnp.float32)
    absorbed = jnp.sum(hit * (phonon_coupling * occupation)[None, :], axis=1)
    emitted = jnp.sum(hit * (phonon_coupling * (occupation + 1.0))[None, :], axis=1)
    lesser = jnp.concatenate([absorbed[::-1], emitted])
    greater = jnp.concatenate([emitted[::-1], absorbed])
    return jnp.stack([lesser, greater])


def sigma_kernel(weights, low, here, high, out):
    energies, rows, columns = here.shape
    taps = [weights[k] for k in range(2 * SHIFT_MAX)]
    offsets = [k - SHIFT_MAX if k < SHIFT_MAX else k - SHIFT_MAX + 1 for k in range(2 * SHIFT_MAX)]
    step, width = 16, 128
    refs = [(low, e) for e in range(SHIFT_MAX)]
    refs += [(here, e) for e in range(energies)]
    refs += [(high, e) for e in range(SHIFT_MAX)]

    def block(position, carry):
        tile = pl.ds(pl.multiple_of(position * step, step), step)
        for left in range(0, columns, width):
            lanes = pl.ds(left, width)
            loaded = [ref[e, tile, lanes].astype(jnp.float32) for ref, e in refs]
            for energy in range(energies):
                terms = [
                    tap * loaded[energy + SHIFT_MAX + offset] for tap, offset in zip(taps, offsets)
                ]
                while len(terms) > 1:
                    terms = [x + y for x, y in zip(terms[0::2], terms[1::2])]
                out[energy, tile, lanes] = terms[0].astype(jnp.bfloat16)
        return carry

    lax.fori_loop(0, rows // step, block, 0)


def self_energy(name, weights, low, here, high, rows, share):
    energies, _, orbitals = here.shape
    halo = pl.BlockSpec((SHIFT_MAX, share, orbitals), lambda r: (0, r, 0))
    full = pl.BlockSpec((energies, share, orbitals), lambda r: (0, r, 0))
    size = energies * rows * orbitals
    return pl.pallas_call(
        sigma_kernel,
        grid=(rows // share,),
        in_specs=[pl.BlockSpec(memory_space=pltpu.SMEM), halo, full, halo],
        out_specs=full,
        out_shape=jax.ShapeDtypeStruct((energies, rows, orbitals), jnp.bfloat16),
        cost_estimate=pl.CostEstimate(flops=16 * size, bytes_accessed=5 * size, transcendentals=0),
        name=f"self_energy_{name}",
    )(weights, low, here, high)


def dot(left, right):
    return jnp.dot(left, right, preferred_element_type=jnp.float32)


def dot_transposed(left, right):
    return lax.dot_general(
        left, right, (((1,), (1,)), ((), ())), preferred_element_type=jnp.float32
    )


def sweep_kernel(first, group, live, lead, sigma, green, coupling, *rest):
    last = rest[1] if first == 0 else None
    out, held, matrix = rest[0] if first == 0 else rest[1], rest[-2], rest[-1]
    narrow = jnp.bfloat16
    orbitals = green.shape[-1]
    rows = coupling.shape[2]
    layer = pl.program_id(0)
    for k, offset in enumerate(ENERGY_OFFSETS):
        start = pl.multiple_of((group[0] ^ offset) * rows, rows)
        matrix[pl.ds(start, rows), :] = coupling[k, 0]

    @pl.when(layer == 0)
    def _():
        held[...] = lead[0]

    row = lax.broadcasted_iota(jnp.int32, (orbitals, orbitals), 0)
    column = lax.broadcasted_iota(jnp.int32, (orbitals, orbitals), 1)
    mask = jnp.maximum(row, column) < live[first + layer]

    v = matrix[...]
    halfway = dot_transposed(held[...], v).astype(narrow)
    share = 4 * orbitals // sigma.shape[0]
    if sigma.shape[1] == share:
        own = sigma[...]
    else:
        own = sigma[:, pl.ds(pl.multiple_of(layer * share, share), share), :]
    own = own.reshape(4 * orbitals, orbitals)
    source = []
    for k in range(4):
        part = slice(k * orbitals, (k + 1) * orbitals)
        spread = dot(v, halfway[part])
        source.append((jnp.where(mask, own[part].astype(jnp.float32), 0.0) + spread).astype(narrow))
    g_real, g_imag = green[0, 0], green[0, 1]
    g_minus = jnp.concatenate([g_real, -g_imag], axis=1)
    g_plus = jnp.concatenate([g_real, g_imag], axis=1)
    for k in (0, 2):
        inner_real = dot(g_minus, jnp.concatenate([source[k], source[k + 1]], axis=0)).astype(narrow)
        inner_imag = dot(g_plus, jnp.concatenate([source[k + 1], source[k]], axis=0)).astype(narrow)
        upper = jnp.concatenate([inner_real, inner_imag], axis=1)
        lower = jnp.concatenate([inner_imag, -inner_real], axis=1)
        outer = dot_transposed(jnp.concatenate([upper, lower], axis=0), g_plus).astype(narrow)
        part = slice(k * orbitals, (k + 2) * orbitals)
        held[part] = outer
        out[0, part] = outer
        if last is not None:
            last[0, part] = outer


def sweep(first, layers, group, live, lead, sigma, green, couplings, whole=None):
    orbitals = green.shape[-1]
    sources, rows, _ = sigma.shape
    share = 4 * orbitals // sources
    count = rows // share
    parts = couplings.shape[0]
    state = pl.BlockSpec((1, 4 * orbitals, orbitals), lambda i, group, live: (0, 0, 0))
    output = pl.BlockSpec((1, 4 * orbitals, orbitals), lambda i, group, live: (first + i, 0, 0))
    operands = [group, live, lead, sigma, green, couplings]
    out_specs, out_shape = [output], [pltpu.HBM((layers, 4 * orbitals, orbitals), jnp.bfloat16)]
    in_specs = [
        state,
        pl.BlockSpec((sources, share, orbitals), lambda i, group, live: (0, i, 0)),
        pl.BlockSpec((1, 2, orbitals, orbitals), lambda i, group, live: (first + i, 0, 0, 0)),
        pl.BlockSpec((parts, 1, orbitals // parts, orbitals), lambda i, group, live: (0, first + i, 0, 0)),
    ]
    if whole is None:
        out_specs.append(state)
        out_shape.append(pltpu.HBM((1, 4 * orbitals, orbitals), jnp.bfloat16))
    else:
        in_specs[1] = pl.BlockSpec(memory_space=pltpu.VMEM)
        in_specs.append(pl.BlockSpec(memory_space=pl.ANY))
        operands.append(whole)
    return pl.pallas_call(
        functools.partial(sweep_kernel, first),
        grid_spec=pltpu.PrefetchScalarGridSpec(
            num_scalar_prefetch=2,
            grid=(count,),
            in_specs=in_specs,
            out_specs=out_specs,
            scratch_shapes=[
                pltpu.VMEM((4 * orbitals, orbitals), jnp.bfloat16),
                pltpu.VMEM((orbitals, orbitals), jnp.bfloat16),
            ],
        ),
        out_shape=out_shape,
        input_output_aliases={} if whole is None else {6: 0},
        cost_estimate=pl.CostEstimate(
            flops=48 * count * orbitals**3,
            bytes_accessed=28 * count * orbitals**2,
            transcendentals=0,
        ),
        compiler_params=pltpu.CompilerParams(vmem_limit_bytes=24 << 20),
        name=f"sweep_{first}",
    )(*operands)


def pick_kernel(blocks, coupling, live, first, second, held, extra, arrived, gone, here, sent):
    layers, devices, share, _ = blocks.shape
    split = first.shape[1] // share
    count = layers - split
    rows = extra.shape[0] - LIVE_ROWS
    start = pl.multiple_of(lax.axis_index("energy") * rows, rows)
    extras = [
        pltpu.make_async_copy(coupling.at[0, pl.ds(start, rows)], extra.at[pl.ds(0, rows)], here.at[0]),
        pltpu.make_async_copy(live, extra.at[pl.ds(rows, LIVE_ROWS)], here.at[1]),
    ]
    tails = [
        pltpu.make_async_copy(extra, second.at[d, pl.ds(count * share, rows + LIVE_ROWS)], sent.at[d])
        for d in range(devices)
    ]
    fetches = [
        pltpu.make_async_copy(blocks.at[split + i], held.at[i], arrived.at[i]) for i in range(count)
    ]
    puts = [
        pltpu.make_async_copy(held.at[i], second.at[:, pl.ds(i * share, share)], gone.at[i])
        for i in range(count)
    ]
    direct = [
        pltpu.make_async_copy(blocks.at[i], first.at[:, pl.ds(i * share, share)], arrived.at[count + i])
        for i in range(split)
    ]
    for copy in extras + fetches + direct:
        copy.start()
    for copy in extras:
        copy.wait()
    for copy in tails:
        copy.start()
    for fetch, put in zip(fetches, puts):
        fetch.wait()
        put.start()
    for copy in direct + tails + puts:
        copy.wait()


def pick(blocks, coupling, live_rows):
    layers, devices, share, orbitals = blocks.shape
    count = layers - FIRST_LAYERS
    extra = orbitals // lax.axis_size("energy") + LIVE_ROWS
    return pl.pallas_call(
        pick_kernel,
        in_specs=[pl.BlockSpec(memory_space=pltpu.HBM)] * 3,
        out_specs=[pl.BlockSpec(memory_space=pltpu.VMEM), pl.BlockSpec(memory_space=pltpu.HBM)],
        out_shape=[
            pltpu.VMEM((devices, FIRST_LAYERS * share, orbitals), blocks.dtype),
            pltpu.HBM((devices, count * share + extra, orbitals), blocks.dtype),
        ],
        scratch_shapes=[
            pltpu.VMEM((count, devices, share, orbitals), blocks.dtype),
            pltpu.VMEM((extra, orbitals), blocks.dtype),
            pltpu.SemaphoreType.DMA((layers,)),
            pltpu.SemaphoreType.DMA((count,)),
            pltpu.SemaphoreType.DMA((2,)),
            pltpu.SemaphoreType.DMA((devices,)),
        ],
        cost_estimate=pl.CostEstimate(flops=0, bytes_accessed=4 * blocks.size, transcendentals=0),
        compiler_params=pltpu.CompilerParams(vmem_limit_bytes=16 << 20),
        name="pick",
    )(blocks, coupling, live_rows)


def settle_kernel(source, out, gone):
    copies = [
        pltpu.make_async_copy(source.at[i], out.at[i], gone.at[i]) for i in range(source.shape[0])
    ]
    for copy in copies:
        copy.start()
    for copy in copies:
        copy.wait()


def settle(blocks):
    return pl.pallas_call(
        settle_kernel,
        in_specs=[pl.BlockSpec(memory_space=pltpu.VMEM)],
        out_specs=pl.BlockSpec(memory_space=pl.ANY),
        out_shape=jax.ShapeDtypeStruct(blocks.shape, blocks.dtype),
        scratch_shapes=[pltpu.SemaphoreType.DMA((blocks.shape[0],))],
        cost_estimate=pl.CostEstimate(flops=0, bytes_accessed=2 * blocks.size, transcendentals=0),
        compiler_params=pltpu.CompilerParams(vmem_limit_bytes=16 << 20),
        name="settle",
    )(blocks)


def exchange(block):
    return lax.all_to_all(block, "layer", split_axis=0, concat_axis=0, tiled=True)


def in_hbm(array):
    return pltpu.with_memory_space_constraint(array, pltpu.HBM)


def exchange_into(block, space):
    return pltpu.with_memory_space_constraint(exchange(block), space)


def halo_of(block):
    count = lax.axis_size("energy")
    forward = [(i, i + 1) for i in range(count - 1)]
    backward = [(i + 1, i) for i in range(count - 1)]
    low = lax.ppermute(block[-SHIFT_MAX:], "energy", forward)
    high = lax.ppermute(block[:SHIFT_MAX], "energy", backward)
    return low, high


def all_couplings(held):
    count = lax.axis_size("energy")
    held = held[None]
    for bit in ENERGY_BITS:
        other = lax.ppermute(held, "energy", [(i, i ^ bit) for i in range(count)])
        held = jnp.concatenate([held, other], axis=0)
    return held


def body(correlations, retarded, coupling, phonon_shifts, phonon_coupling, layer_orbitals):
    layers, parts, orbitals = correlations.shape[1:4]
    devices = lax.axis_size("layer")
    share = parts * orbitals // devices
    pair = lax.axis_index("layer") * 2 // devices
    weights = lax.dynamic_index_in_dim(tap_weights(phonon_shifts, phonon_coupling), pair, 0, keepdims=False)
    group = lax.axis_index("energy").astype(jnp.int32)[None]
    live_rows = jnp.broadcast_to(layer_orbitals.astype(jnp.bfloat16)[:, None], (LIVE_ROWS, orbitals))
    blocks = correlations.reshape(layers, devices, share, orbitals)
    picked = pick(in_hbm(blocks), in_hbm(coupling), live_rows)
    arrived = [exchange(block) for block in picked]
    rows = (FIRST_LAYERS * share, (layers - FIRST_LAYERS) * share)
    extra = arrived[1][:, rows[1] :]
    group_rows = extra.shape[1] - LIVE_ROWS
    couplings = all_couplings(extra[:, :group_rows])
    live = extra[:, group_rows, 0].astype(jnp.int32)
    sigmas = []
    for c in range(2):
        low, high = halo_of(arrived[c][:, : rows[c]])
        sigmas.append(self_energy(c, weights, low, arrived[c], high, rows[c], 2 * share))
    sigmas[1], couplings, live = lax.optimization_barrier((sigmas[1], couplings, live))
    lead = in_hbm(correlations.reshape(layers, parts * orbitals, orbitals))
    green, couplings = in_hbm(retarded[0]), in_hbm(couplings)
    spaces = (pltpu.HBM, pltpu.VMEM)
    returned = [exchange_into(sigma, space) for sigma, space in zip(sigmas, spaces)]
    whole, lead = sweep(0, layers, group, live, lead, returned[0], green, couplings)
    (whole,) = sweep(FIRST_LAYERS, layers, group, live, in_hbm(lead), returned[1], green, couplings, whole)
    return settle(exchange_into(whole, pltpu.VMEM)).reshape(layers, 1, parts, orbitals, orbitals)


def solution(mesh):
    return jax.shard_map(
        body,
        mesh=mesh,
        in_specs=(
            P(("energy", "layer"), None, None, None, None),
            P(("energy", "layer"), None, None, None, None),
            P("layer", None, None),
            P(),
            P(),
            P("layer"),
        ),
        out_specs=P("energy", "layer", None, None, None),
        check_vma=False,
    )
```
